256 devices in a mesh: sec: 4 (over x), tile: 64 (over y, z, core).
Axes of the slice: x: 4, y: 4, z: 8, core: 2. Of those that a mesh axis runs over, the one named last changes fastest.
Arguments:
- patches: bfloat16 [4, 256, 512, 512], P('sec', 'tile'), may hold values from -6 to 6
- zoom: float32 [4, 2, 256], P('sec'), may hold values from 0.75 to 0.9
- frac: float32 [4, 2, 256], P('sec'), may hold values from 0 to 1
- offset: int32 [4, 2, 256], P('sec'), may hold values from 0 to 15
- owner: int32 [4, 256, 16, 1], P('sec'), may hold values from 0 to 63; in each aligned block of 64 rows (0 to 63, 64 to 127, ..., all dimensions but the last counted through in order) at most 2 rows name the same one
- top_grid: bfloat16 [64, 256, 256], P('tile'), may hold values from -3 to 3
Outputs:
- grid_image: bfloat16 [4, 64, 256, 256], P('sec', 'tile')
- corrections: float32 [6, 4, 256], P(None, 'sec', 'tile')
The draws below stay inside these ranges and needn't reach their ends.
Inputs may be any that keep to these rules, and one draw needn't show every extreme that they name: `owner`: in each section, the bands of one device's 4 tiles (aligned blocks of 64 rows) name no grid tile more than 2 times; in some blocks one grid tile is named exactly 2 times.
All inputs are finite; a program needn't handle non-finite values.
Results may differ from the reference program's by a relative error of at most 0.0018.
The reference program's roundings to bfloat16 on the way count: a program that leaves them out, or rounds other values in their place, can miss the bound.
Values may be sent and summed in bfloat16 or wider, within the bound.
A program may use at most 64 MiB of HBM per device.

```python
import math
import jax
import jax.numpy as jnp
import numpy as np
from jax import lax

P_SIZE = 512
Q = 256
BAND = 16
NB = 16
TILE_DEV = 4
ITERS = 2
CAP = 2
SECTIONS = 4
TILES = 256
GRID = 64
N_TILE = 64


def plant(values, own_key, smallest, top_value):
    spot = [jax.random.randint(jax.random.fold_in(own_key, axis), (), 0, length) for axis, length in enumerate(values.shape)]
    main_axis = values.shape.index(max(values.shape))
    beside = spot[:main_axis] + [(spot[main_axis] + 1) % values.shape[main_axis]] + spot[main_axis + 1:]
    return values.at[tuple(spot)].set(smallest).at[tuple(beside)].set(top_value)


def level_of(own_key, shape, shards, low, top_value):
    def one(position, blocks):
        steps = jax.random.uniform(jax.random.fold_in(jax.random.fold_in(own_key, 6), position), (blocks,), jnp.float32, low / len(shards), top_value / len(shards))
        return jnp.repeat(jnp.exp(steps), shape[position] // blocks).reshape((-1,) + (1,) * (len(shape) - position - 1))

    loudness = one(*shards[0])
    for cut in shards[1:]:
        loudness = loudness * one(*cut)
    return loudness


def assign_block(key, own, number, rows, count, top, limit, slope):
    sequence = jax.random.permutation(key, count)
    crowded, usual = shares(count, rows * top, limit, slope, True), shares(count, rows * top, limit, slope, False)
    places = jnp.arange(count)

    def named(tallies, offset_by):
        used = int((tallies > 0).sum())
        fixed = max(1, used // 4)
        moved = fixed + (places - fixed + offset_by * (used - fixed)) % max(1, count - fixed)
        return jnp.zeros((count,), jnp.int32).at[sequence[jnp.where(places < fixed, places, moved)]].set(jnp.asarray(tallies, jnp.int32))

    tallies = jnp.where(number % 4 == 0, named(crowded, number // 4), named(usual, number - number // 4 - 1))
    mixed = jax.random.permutation(jax.random.fold_in(own, 3), count)
    source_of, taker = mixed[0:count // 2 * 2:2], mixed[1:count // 2 * 2:2]
    slack = jnp.minimum(tallies[source_of] - 1, limit - tallies[taker]) // 2
    slack = jnp.where((source_of == sequence[0]) | (taker == sequence[0]) | (tallies[taker] == 0), 0, jnp.maximum(slack, 0))
    moved = jax.random.randint(jax.random.fold_in(own, 4), (count // 2,), 0, 1 << 20) % (slack + 1)
    tallies = tallies.at[source_of].add(-moved).at[taker].add(moved)
    labels = jnp.searchsorted(jnp.cumsum(tallies), jnp.arange(rows * top), side="right").astype(jnp.int32)
    grid = labels.reshape(top, rows).T
    grid = grid[jax.random.permutation(jax.random.fold_in(own, 1), rows)]
    offset_by = jax.random.randint(jax.random.fold_in(own, 2), (rows, 1), 0, top)
    return jnp.take_along_axis(grid, (jnp.arange(top)[None, :] + offset_by) % top, axis=1)


def shares(amount, total, reach, slope, full):
    portions = [(1 << 20) // math.isqrt(standing ** slope) + 1 for standing in range(1, amount + 1)]
    largest = reach if full else min(reach, max(-(-total // amount), total * portions[0] // sum(portions)))
    least = 1 if total - largest >= amount - 1 else 0
    given, rest = [largest] + [least] * (amount - 1), total - largest - least * (amount - 1)
    while rest > 0:
        free = [i for i in range(1, amount) if given[i] < largest] or [i for i in range(1, amount) if given[i] < reach]
        whole, remaining = sum([portions[i] for i in free]), rest
        for i in free:
            extra = min(reach - given[i], max(1, remaining * portions[i] // whole), rest)
            given[i] = given[i] + extra
            rest = rest - extra
    return np.array(given)


def normal_values(key, extent, deviation, most, split=(), kind=jnp.bfloat16):
    values = jax.random.normal(key, extent, jnp.float32) * deviation
    if len(split) > 0:
        values = level_of(key, extent, split, -0.22, 0.18) * values
    return jnp.clip(values, min=-most, max=most).astype(kind)


def setup_inputs(seed: int = 0) -> dict:
    streams_of = jax.random.split(jax.random.key(seed), 7)
    patches = normal_values(streams_of[0], (SECTIONS, TILES, P_SIZE, P_SIZE), 1.0, 6.0, ((0, 4), (1, 64)))
    zoom = jnp.clip(0.75 + 0.14999998 * jax.random.uniform(streams_of[1], (SECTIONS, 2, TILES), jnp.float32) ** level_of(streams_of[1], (SECTIONS, 2, TILES), ((0, 4),), -0.2, 0.2), 0.75, 0.9)
    frac = jnp.clip(1.0 * jax.random.uniform(streams_of[2], (SECTIONS, 2, TILES), jnp.float32) ** level_of(streams_of[2], (SECTIONS, 2, TILES), ((0, 4),), -0.2, 0.2), 0.0, 1.0)
    offset = plant(jax.random.randint(streams_of[3], (SECTIONS, 2, TILES), 0, Q // 16), jax.random.fold_in(streams_of[3], 1), 0, (Q // 16) - 1).astype(jnp.int32)
    owner_keys = jax.random.split(jax.random.fold_in(streams_of[4], 1), SECTIONS * TILES * NB // (TILE_DEV * NB))
    owner_turns = jax.random.permutation(jax.random.fold_in(streams_of[4], 3), SECTIONS * TILES * NB // (TILE_DEV * NB))
    owner = jax.vmap(lambda own, number: assign_block(jax.random.fold_in(streams_of[4], 2), own, number, TILE_DEV * NB, N_TILE, 1, CAP, 2))(owner_keys, owner_turns).reshape((SECTIONS, TILES, NB, 1))
    top_grid = normal_values(streams_of[5], (GRID, Q, Q), 0.4, 3.0, ((0, 64),))
    return {"patches": patches, "zoom": zoom, "frac": frac, "offset": offset, "owner": owner, "top_grid": top_grid}


COUPLING = 0.25


def hat_weight(distance):
    return jnp.maximum(0.0, 1.0 - jnp.abs(distance))


def sample_points(zoom, frac, offset, frame, source):
    scale = zoom * (frame / source)
    spots = jnp.arange(frame, dtype=jnp.float32)
    return (spots - offset.astype(jnp.float32)[..., None] - frac[..., None]) / scale[..., None]


def coverage(points, source):
    return jnp.clip(jnp.minimum(points + 1.0, source - points), 0.0, 1.0)


def moments(intensity, target, row_cover, col_cover, row_pos, frame):
    middle = (frame - 1) / 2.0
    level = intensity.astype(jnp.float32)
    error = target.astype(jnp.float32) - level
    weight = row_cover[:, :, None] * col_cover[:, None, :] / (frame * frame)
    columns = (jnp.arange(frame, dtype=jnp.float32) - middle) / (frame / 2.0)
    row_coord = (row_pos - middle) / (frame / 2.0)
    x_grid = jnp.broadcast_to(columns[None, None, :], level.shape)
    y_grid = jnp.broadcast_to(row_coord[:, :, None], level.shape)
    features = jnp.stack([jnp.ones_like(level), x_grid, y_grid, level, level * x_grid, level * y_grid], axis=1)
    weighted = features * weight[:, None]
    normal = jnp.einsum("bfrq,bgrq->bfg", weighted, features, precision=lax.Precision.HIGHEST)
    gradient = jnp.einsum("bfrq,brq->bf", weighted, error, precision=lax.Precision.HIGHEST)
    return normal, gradient


def blocked_moments(intensity, target, row_cover, col_cover, row_pos, frame):
    count = intensity.shape[0]
    block_size = math.gcd(count, 64)

    def block_moments(block_args):
        return moments(block_args[0], block_args[1], block_args[2], block_args[3], block_args[4], frame)

    shaped = tuple(member.reshape((count // block_size, block_size) + member.shape[1:]) for member in (intensity, target, row_cover, col_cover, row_pos))
    normal, gradient = lax.map(block_moments, shaped)
    return normal.reshape(count, 6, 6), gradient.reshape(count, 6)


def tap_pair(points, source):
    base = jnp.floor(points)
    lower = base.astype(jnp.int32)
    upper = lower + 1
    weight_lower = jnp.where((lower >= 0) & (lower < source), hat_weight(points - base), 0.0).astype(jnp.bfloat16)
    weight_upper = jnp.where((upper >= 0) & (upper < source), hat_weight(points - (base + 1.0)), 0.0).astype(jnp.bfloat16)
    return jnp.clip(lower, 0, source - 1), jnp.clip(upper, 0, source - 1), weight_lower, weight_upper


def render_tile(patch, row_points, col_points):
    row_lower, row_upper, row_wlow, row_wup = tap_pair(row_points, P_SIZE)
    halfway = (row_wlow.astype(jnp.float32)[:, None] * patch[row_lower].astype(jnp.float32)
               + row_wup.astype(jnp.float32)[:, None] * patch[row_upper].astype(jnp.float32)).astype(jnp.bfloat16)
    col_lower, col_upper, col_wlow, col_wup = tap_pair(col_points, P_SIZE)
    return (halfway[:, col_lower].astype(jnp.float32) * col_wlow.astype(jnp.float32)[None, :]
            + halfway[:, col_upper].astype(jnp.float32) * col_wup.astype(jnp.float32)[None, :]).astype(jnp.bfloat16)


def reference(patches, zoom, frac, offset, owner, top_grid):
    bands = Q // BAND
    points = sample_points(zoom, frac, offset, Q, P_SIZE)
    covered = coverage(points, P_SIZE)
    routes = owner[..., 0]

    def render_section(section_args):
        patch_set, point_set = section_args
        return jax.vmap(render_tile)(patch_set, point_set[0], point_set[1])

    rendered = lax.map(render_section, (patches, points))
    band_ids = jnp.arange(bands, dtype=jnp.int32)

    def grid_section(section_args):
        frames, route_set, cover_set = section_args
        segment = (route_set * bands + band_ids[None, :]).reshape(TILES * bands)
        band_stack = frames.reshape(TILES * bands, BAND * Q).astype(jnp.float32)
        image_sum = jax.ops.segment_sum(band_stack, segment, num_segments=GRID * bands)
        row_bands = cover_set[0].reshape(TILES * bands, BAND)
        col_rows = jnp.repeat(cover_set[1], bands, axis=0)
        products = (row_bands[:, :, None] * col_rows[:, None, :]).reshape(TILES * bands, BAND * Q)
        cover_sum = jax.ops.segment_sum(products, segment, num_segments=GRID * bands)
        return (image_sum / (1.0 + cover_sum)).astype(jnp.bfloat16).reshape(GRID, Q, Q)

    grid_image = lax.map(grid_section, (rendered, routes, covered))
    above_all = jnp.concatenate([grid_image[1:], top_grid[None]], axis=0)
    row_spots = jnp.arange(BAND, dtype=jnp.float32)
    row_pos = ((jnp.arange(TILES * bands, dtype=jnp.int32) % bands).astype(jnp.float32) * BAND)[:, None] + row_spots

    def normal_section(section_args):
        frames, route_set, cover_set, target_grid = section_args
        segment = (route_set * bands + band_ids[None, :]).reshape(TILES * bands)
        target = target_grid.reshape(GRID * bands, BAND, Q)[segment]
        row_bands = cover_set[0].reshape(TILES * bands, BAND)
        col_rows = jnp.repeat(cover_set[1], bands, axis=0)
        normal, gradient = blocked_moments(frames.reshape(TILES * bands, BAND, Q), target, row_bands, col_rows, row_pos, Q)
        return normal.reshape(TILES, bands, 6, 6).sum(axis=1), gradient.reshape(TILES, bands, 6).sum(axis=1)

    normals, gradients = lax.map(normal_section, (rendered, routes, covered, above_all))
    right_side = jnp.transpose(gradients, (2, 0, 1))
    diagonal_part = jnp.transpose(jnp.diagonal(normals, axis1=2, axis2=3), (2, 0, 1))
    precond = 1.0 / (diagonal_part + 4.0 * COUPLING)

    def apply_system(vector):
        padded = jnp.pad(vector, ((0, 0), (1, 1), (1, 1)))
        beside = padded[:, 2:, 1:-1] + padded[:, :-2, 1:-1] + padded[:, 1:-1, 2:] + padded[:, 1:-1, :-2]
        return jnp.einsum("stfg,gst->fst", normals, vector, precision=lax.Precision.HIGHEST) + COUPLING * (4.0 * vector - beside)

    solution = jnp.zeros_like(right_side)
    residual = right_side
    scaled = precond * residual
    direction = scaled
    current = jnp.sum(residual * scaled)
    for step in range(ITERS):
        image = apply_system(direction)
        alpha = current / jnp.sum(direction * image)
        solution = solution + alpha * direction
        if step + 1 < ITERS:
            residual = residual - alpha * image
            scaled = precond * residual
            following = jnp.sum(residual * scaled)
            direction = scaled + (following / current) * direction
            current = following
    return grid_image, solution
```

```python
import functools

import jax
import jax.numpy as jnp
from jax import lax
from jax.experimental import pallas as pl
from jax.experimental.pallas import tpu as pltpu
from jax.sharding import PartitionSpec as P

BAND = 16
ITERS = 2
COUPLING = 0.25
MESH = pl.DeviceIdType.MESH
F32 = jnp.float32
BF16 = jnp.bfloat16

MONOMIALS = ((0, 0), (1, 0), (0, 1), (2, 0), (1, 1), (0, 2))
PAIR = ((0, 1, 2), (1, 3, 4), (2, 4, 5))
GRADS = 6


def moment_of(f, g):
    return (f // 3 + g // 3) * 6 + PAIR[f % 3][g % 3]


def iota(shape, dim):
    return lax.broadcasted_iota(jnp.int32, shape, dim)


def fiota(shape, dim):
    return iota(shape, dim).astype(F32)


def shifted(x, distance):
    width = x.shape[1]
    return pltpu.roll(x, (-distance) % width, 1)


def total(x):
    return jnp.sum(jnp.sum(x, axis=0, keepdims=True), axis=1, keepdims=True)


def kernel(
    sections, devices, tiles, source, frame,
    zoom_hbm, frac_hbm, offset_hbm, routes_hbm, patch_hbm, top_hbm,
    grid_hbm, corr_ref,
    zoom_s, frac_s, offset_s, tab_s, tab_v, routes_v,
    patch_v, rendered, outgoing, incoming, weights, weights_hi, weights_lo, lit,
    select, grid_v, above, partial, values, returned, returning,
    payload, gathered_pair, chip_rows, gathered, planes,
    param_sem, route_sem, patch_sem, tab_sem, top_sem, out_sem,
    send_a, recv_a, send_g, recv_g, send_r, recv_r, send_p, recv_p, send_c, recv_c,
):
    bands = frame // BAND
    rows = tiles * bands
    me_sec = lax.axis_index("sec")
    me = lax.axis_index("tile")
    chip, core = me // 2, me % 2
    chips = devices // 2
    half = frame // 2
    middle = (frame - 1) / 2.0

    params = [
        pltpu.make_async_copy(a, b, param_sem.at[n])
        for n, (a, b) in enumerate(((zoom_hbm, zoom_s), (frac_hbm, frac_s), (offset_hbm, offset_s)))
    ]
    route_copy = pltpu.make_async_copy(routes_hbm, routes_v, route_sem)
    route_copy.start()
    for c in params:
        c.start()

    def patch_copy(t):
        return pltpu.make_async_copy(patch_hbm.at[t], patch_v.at[t], patch_sem.at[t])

    for t in range(tiles):
        patch_copy(t).start()
    top_copy = pltpu.make_async_copy(top_hbm, above, top_sem)

    @pl.when(me_sec == sections - 1)
    def _():
        top_copy.start()

    barrier = pltpu.get_barrier_semaphore()

    def greet(d, carry):
        pl.semaphore_signal(
            barrier, 1, device_id=(me_sec, lax.rem(me + d, devices)), device_id_type=MESH
        )
        return carry

    lax.fori_loop(1, devices, greet, 0)
    pair_peers = [
        (lax.rem(me_sec + ds, sections), chip * 2 + lax.rem(core + dc, 2))
        for ds in range(sections)
        for dc in range(2)
        if ds or dc
    ]
    for n, peer in enumerate(pair_peers):
        if n:
            pl.semaphore_signal(barrier, 1, device_id=peer, device_id_type=MESH)

    route_copy.wait()
    lane = iota((devices, 128), 1)
    mine = (routes_v[...] == me) & (lane < rows)
    take0 = jnp.min(jnp.where(mine, lane, rows - 1), axis=1, keepdims=True)
    take1 = jnp.max(jnp.where(mine, lane, 0), axis=1, keepdims=True)
    count = jnp.sum(jnp.where(mine, 1, 0), axis=1, keepdims=True)
    own_row = routes_v[pl.ds(me, 1), :]
    hit = (own_row == iota((devices, 128), 0)) & (lane < rows)
    out0 = jnp.min(jnp.where(hit, lane, rows - 1), axis=1, keepdims=True)
    out1 = jnp.max(jnp.where(hit, lane, 0), axis=1, keepdims=True)
    valid0 = count > 0
    valid1 = count > 1
    idx0, idx1 = take0, take1
    on0 = valid0.astype(jnp.int32)
    on1 = valid1.astype(jnp.int32)
    table = jnp.where(lane == 0, idx0, 0)
    table = jnp.where(lane == 1, idx1, table)
    table = jnp.where(lane == 2, out0, table)
    table = jnp.where(lane == 3, out1, table)
    table = jnp.where(lane == 4, on0, table)
    table = jnp.where(lane == 5, on1, table)
    tab_v[...] = table
    tab_copy = pltpu.make_async_copy(tab_v, tab_s, tab_sem)
    tab_copy.start()
    for c in params:
        c.wait()

    def scale_of(a, i):
        return zoom_s[a, i] * (frame / source)

    def points_of(spots, a, i):
        return (spots - offset_s[a, i].astype(F32) - frac_s[a, i]) / scale_of(a, i)

    def cover_of(points):
        return jnp.clip(jnp.minimum(points + 1.0, source - points), 0.0, 1.0)

    def hat(distance):
        return jnp.maximum(0.0, 1.0 - jnp.abs(distance)).astype(BF16)

    def render(t, carry):
        i = me * tiles + t
        down = points_of(fiota((frame, 128), 0), 0, i)
        down = jnp.concatenate([down] * (source // 128), axis=1)
        row_weights = hat(down - fiota((frame, source), 1))
        across = points_of(fiota((8, frame), 1), 1, i)
        across = jnp.broadcast_to(across[0:1], (source, frame))
        col_weights = hat(across - fiota((source, frame), 0))
        patch_copy(t).wait()
        halfway = jnp.dot(row_weights, patch_v[t], preferred_element_type=F32).astype(BF16)
        image = jnp.dot(halfway, col_weights, preferred_element_type=F32).astype(BF16)
        rendered[pl.ds(pl.multiple_of(t * bands, bands), bands)] = image.reshape(bands, BAND, frame)
        return carry

    lax.fori_loop(0, tiles, render, 0)

    tab_copy.wait()

    def pack(g, carry):
        outgoing[g, 0] = rendered[tab_s[g, 2] & (rows - 1)]
        outgoing[g, 1] = rendered[tab_s[g, 3] & (rows - 1)]
        return carry

    lax.fori_loop(0, devices, pack, 0)
    incoming[me] = outgoing[me]
    greeted = devices - 1 + len(pair_peers) - 1
    pl.semaphore_wait(barrier, greeted)

    def band_copy(peer, from_):
        return pltpu.make_async_remote_copy(
            src_ref=outgoing.at[peer],
            dst_ref=incoming.at[from_],
            send_sem=send_a.at[peer],
            recv_sem=recv_a.at[from_],
            device_id=(me_sec, peer),
            device_id_type=MESH,
        )

    def send_bands(d, carry):
        band_copy(lax.rem(me + d, devices), me).start()
        return carry

    lax.fori_loop(1, devices, send_bands, 0)

    def cover_slot(j, carry):
        for c in range(2):
            idx = tab_s[j, c] & (rows - 1)
            i = j * tiles + (idx >> 4)
            k = idx & (bands - 1)
            start = (k * BAND).astype(F32)
            down = cover_of(points_of(fiota((BAND, 128), 0) + start, 0, i))
            down = down * (tab_s[j, 4 + c].astype(F32) / (frame * frame))
            across = cover_of(points_of(fiota((8, frame), 1), 1, i))
            weight = jnp.concatenate([down, down], axis=1) * jnp.broadcast_to(
                across[0:1], (BAND, frame)
            )
            weights[j, c] = weight
            hi = weight.astype(BF16)
            weights_hi[j, c] = hi
            weights_lo[j, c] = (weight - hi.astype(F32)).astype(BF16)
        return carry

    lax.fori_loop(0, devices, cover_slot, 0)

    sub = iota((devices, 128), 0)
    band0 = jnp.where(valid0, (idx0 & (bands - 1)).astype(F32), -float(bands))
    band1 = jnp.where(valid1, (idx1 & (bands - 1)).astype(F32), -float(bands))
    along = jnp.where(lane == sub, band0, 0.0) + jnp.where(lane == sub + devices, band1, 0.0)
    along = jnp.broadcast_to(jnp.sum(along, axis=0, keepdims=True), (8, 128)).astype(BF16)
    chunk = 256 // (2 * BAND)
    chunks = devices // chunk
    wide = iota((128, 256), 1)

    def choose(h, cover):
        spread = (iota((128, 256), 0) == h * chunk + wide // (2 * BAND) + devices * ((wide // BAND) % 2))
        spread = jnp.where(spread, 1.0, 0.0).astype(BF16)
        target = jnp.dot(along, spread, preferred_element_type=F32)[0:1]
        target = target * BAND + (iota((1, 256), 1) % BAND).astype(F32)
        onehot = jnp.where(fiota((frame, 256), 0) == target, 1.0, 0.0).astype(BF16)
        select[h] = onehot
        at = pl.ds(pl.multiple_of(h * chunk, chunk), chunk)
        cover += jnp.dot(onehot, weights_hi[at].reshape(256, frame), preferred_element_type=F32)
        cover += jnp.dot(onehot, weights_lo[at].reshape(256, frame), preferred_element_type=F32)
        return cover

    cover = lax.fori_loop(0, chunks, choose, jnp.zeros((frame, frame), F32))
    cover = 1.0 + cover * float(frame * frame)

    row_lane = iota((1, 128), 1)

    def moments(t, payload):
        i = me * tiles + t
        down = cover_of(points_of(fiota((frame, 128), 0), 0, i)) / (frame * frame)
        y = (fiota((frame, 128), 0) - middle) / (frame / 2.0)
        down = [jnp.concatenate([v, v], axis=1) for v in (down, down * y, down * y * y)]
        across = cover_of(points_of(fiota((8, frame), 1), 1, i))[0:1]
        x = (fiota((1, frame), 1) - middle) / (frame / 2.0)
        across = (across, across * x, across * x * x)
        at = pl.ds(pl.multiple_of(t * bands, bands), bands)
        level = rendered[at].reshape(frame, frame).astype(F32)
        for p, image in enumerate((None, level, level * level)):
            for b in range(3):
                column = down[b] if image is None else down[b] * image
                column = jnp.sum(column, axis=0, keepdims=True)
                for m, (a, b2) in enumerate(MONOMIALS):
                    if b2 == b:
                        value = jnp.sum(column * across[a], axis=1, keepdims=True)
                        payload = jnp.where(
                            row_lane == GRADS * tiles + (p * 6 + m) * tiles + t, value, payload
                        )
                        if p >= 1 and (a + b) <= 1:
                            payload = jnp.where(
                                row_lane == ((p - 1) * 3 + m) * tiles + t, -value, payload
                            )
        return payload

    own = lax.fori_loop(0, tiles, moments, jnp.zeros((1, 128), F32))

    grid = jnp.zeros((frame, frame), F32)

    def arrive(h, grid):
        def one(n, carry):
            j = h * chunk + n

            @pl.when(j != me)
            def _():
                band_copy(j, j).wait_recv()

            return carry

        lax.fori_loop(0, chunk, one, 0)
        at = pl.ds(pl.multiple_of(h * chunk, chunk), chunk)
        return grid + jnp.dot(
            select[h], incoming[at].reshape(256, frame), preferred_element_type=F32
        )

    grid = lax.fori_loop(0, chunks, arrive, grid)
    grid_v[...] = (grid / cover).astype(BF16).reshape(bands, BAND, frame)
    write_grid = pltpu.make_async_copy(grid_v, grid_hbm, out_sem)
    write_grid.start()
    to_below = pltpu.make_async_remote_copy(
        src_ref=grid_v,
        dst_ref=above,
        send_sem=send_g,
        recv_sem=recv_g,
        device_id=(lax.rem(me_sec + sections - 1, sections), me),
        device_id_type=MESH,
    )

    @pl.when(me_sec > 0)
    def _():
        to_below.start()

    def weigh(j, carry):
        for c in range(2):
            lit[j, c] = weights[j, c] * incoming[j, c].astype(F32)
        return carry

    lax.fori_loop(0, devices, weigh, 0)

    @pl.when(me_sec < sections - 1)
    def _():
        to_below.wait_recv()

    @pl.when(me_sec == sections - 1)
    def _():
        top_copy.wait()

    x = (fiota((8, frame), 1) - middle) / (frame / 2.0)
    x0, x1 = x[:, :half], x[:, half:]
    y_base = (fiota((BAND, half), 0) - middle) / (frame / 2.0)

    def contract(j, carry):
        for c in range(2):
            k = tab_s[j, c] & (bands - 1)
            target = above[k].astype(F32)
            y = y_base + (k * BAND).astype(F32) / (frame / 2.0)
            for n, factor in enumerate((weights, lit)):
                product = target * factor[j, c]
                left, right = product[:, :half], product[:, half:]
                both = left + right
                left, right = left[:8] + left[8:], right[:8] + right[8:]
                y_part = both * y
                partial[c, n * 3, j] = left + right
                partial[c, n * 3 + 1, j] = left * x0 + right * x1
                partial[c, n * 3 + 2, j] = y_part[:8] + y_part[8:]
        return carry

    lax.fori_loop(0, devices, contract, 0)
    answer = jnp.zeros((devices, 128), F32)
    for c, (idx, valid) in enumerate(((idx0, valid0), (idx1, valid1))):
        tile_of = jnp.where(valid, idx // bands, -1)
        for f in range(GRADS):
            value = jnp.sum(jnp.sum(partial[c, f], axis=1), axis=1, keepdims=True)
            answer = answer + jnp.where(lane == f * tiles + tile_of, value, 0.0)
    values[...] = answer

    def unfold(j, carry):
        returned[j] = values[pl.ds(j, 1), :]
        return carry

    lax.fori_loop(0, devices, unfold, 0)
    returning[me] = returned[me]

    def sum_copy(peer, from_):
        return pltpu.make_async_remote_copy(
            src_ref=returned.at[peer],
            dst_ref=returning.at[from_],
            send_sem=send_r.at[peer],
            recv_sem=recv_r.at[from_],
            device_id=(me_sec, peer),
            device_id_type=MESH,
        )

    def send_sums(d, carry):
        sum_copy(lax.rem(me + d, devices), me).start()
        return carry

    lax.fori_loop(1, devices, send_sums, 0)

    def await_sums(d, carry):
        j = lax.rem(me + d, devices)
        sum_copy(j, j).wait_recv()
        return carry

    lax.fori_loop(1, devices, await_sums, 0)
    own = own + jnp.sum(returning[...], axis=0)

    payload[...] = own
    place = me_sec * 2 + core
    gathered_pair[place] = own

    def pair_copy(n, peer, from_):
        return pltpu.make_async_remote_copy(
            src_ref=payload,
            dst_ref=gathered_pair.at[from_],
            send_sem=send_p.at[n],
            recv_sem=recv_p.at[from_],
            device_id=peer,
            device_id_type=MESH,
        )

    for n, peer in enumerate(pair_peers):
        pair_copy(n, peer, place).start()
    for n, peer in enumerate(pair_peers):
        pair_copy(n, peer, peer[0] * 2 + lax.rem(peer[1], 2)).wait_recv()
    for n in range(2 * sections):
        chip_rows[n : n + 1, :] = gathered_pair[n]
    gathered[chip] = chip_rows[...]

    def chip_copy(other, from_):
        return pltpu.make_async_remote_copy(
            src_ref=chip_rows,
            dst_ref=gathered.at[from_],
            send_sem=send_c.at[other],
            recv_sem=recv_c.at[from_],
            device_id=(me_sec, other * 2 + core),
            device_id_type=MESH,
        )

    def send_rows(d, carry):
        chip_copy(lax.rem(chip + d, chips), chip).start()
        return carry

    lax.fori_loop(1, chips, send_rows, 0)

    def await_rows(d, carry):
        j = lax.rem(chip + d, chips)
        chip_copy(j, j).wait_recv()
        return carry

    lax.fori_loop(1, chips, await_rows, 0)
    everyone = 2 * sections * chips
    planes[...] = jnp.transpose(gathered[...].reshape(everyone, 128))

    shape = (8, everyone)
    lane_id = iota(shape, 1)
    tile_id = iota(shape, 0)
    pairs = 2 * sections
    lane_chip, lane_sec, lane_core = lane_id // pairs, (lane_id % pairs) // 2, lane_id % 2
    used = tile_id < tiles
    right_side = [
        jnp.where(used, planes[f * tiles : f * tiles + 8, :], 0.0) for f in range(GRADS)
    ]
    moment = [
        planes[(GRADS + m) * tiles : (GRADS + m) * tiles + 8, :] for m in range(18)
    ]
    precond = [
        jnp.where(used, 1.0 / (moment[moment_of(f, f)] + 4.0 * COUPLING), 0.0) for f in range(GRADS)
    ]
    has_next = ~((lane_chip == chips - 1) & (lane_core == 1)) | (tile_id < tiles - 1)
    has_before = ~((lane_chip == 0) & (lane_core == 0)) | (tile_id > 0)

    def beside_of(d):
        up = pltpu.roll(d, 7, 0)
        over = pltpu.roll(d, tiles - 1, 0)
        over = jnp.where(lane_core == 0, shifted(over, 1), shifted(over, pairs - 1))
        after = jnp.where(used & has_next, jnp.where(tile_id == tiles - 1, over, up), 0.0)
        down = pltpu.roll(d, 1, 0)
        under = pltpu.roll(d, 8 - (tiles - 1), 0)
        under = jnp.where(lane_core == 1, shifted(under, -1), shifted(under, 1 - pairs))
        before = jnp.where(used & has_before, jnp.where(tile_id == 0, under, down), 0.0)
        upper = jnp.where(lane_sec < sections - 1, shifted(d, 2), 0.0)
        lower = jnp.where(lane_sec > 0, shifted(d, -2), 0.0)
        return upper + lower + after + before

    def inner(left, right):
        return total(sum(a * b for a, b in zip(left, right)))

    residual = right_side
    scaled = [p * r for p, r in zip(precond, residual)]
    direction = scaled
    current = inner(residual, scaled)
    result = [jnp.zeros(shape, F32)] * GRADS
    for step in range(ITERS):
        image = [
            sum(moment[moment_of(f, g)] * direction[g] for g in range(GRADS))
            + COUPLING * (4.0 * direction[f] - beside_of(direction[f]))
            for f in range(GRADS)
        ]
        alpha = current / inner(direction, image)
        result = [c + alpha * d for c, d in zip(result, direction)]
        if step + 1 < ITERS:
            residual = [r - alpha * h for r, h in zip(residual, image)]
            scaled = [p * r for p, r in zip(precond, residual)]
            following = inner(residual, scaled)
            ratio = following / current
            direction = [z + ratio * d for z, d in zip(scaled, direction)]
            current = following
    my_lane = chip * pairs + place
    for f in range(GRADS):
        column = jnp.sum(jnp.where(lane_id == my_lane, result[f], 0.0), axis=1, keepdims=True)
        turned = jnp.where(iota((8, 128), 0) == iota((8, 128), 1), column, 0.0)
        corr_ref[f] = jnp.sum(turned, axis=0, keepdims=True)[:, :tiles]

    def sent(d, carry):
        peer = lax.rem(me + d, devices)
        band_copy(peer, me).wait_send()
        sum_copy(peer, me).wait_send()
        return carry

    lax.fori_loop(1, devices, sent, 0)

    def sent_rows(d, carry):
        chip_copy(lax.rem(chip + d, chips), chip).wait_send()
        return carry

    lax.fori_loop(1, chips, sent_rows, 0)
    for n, peer in enumerate(pair_peers):
        pair_copy(n, peer, place).wait_send()

    @pl.when(me_sec > 0)
    def _():
        to_below.wait_send()

    write_grid.wait()


def shards(patches, zoom, frac, offset, owner, top_grid):
    _, tiles, source, _ = patches.shape
    frame = top_grid.shape[1]
    sections, devices = lax.axis_size("sec"), lax.axis_size("tile")
    bands = frame // BAND
    rows = tiles * bands
    chips = devices // 2
    pairs = 2 * sections
    routes = jnp.pad(owner.reshape(devices, rows), ((0, 0), (0, 128 - rows)))
    any_space = pl.BlockSpec(memory_space=pl.ANY)
    vmem, smem, sem = pltpu.VMEM, pltpu.SMEM, pltpu.SemaphoreType.DMA
    all_tiles = tiles * devices
    grid, corrections = pl.pallas_call(
        functools.partial(kernel, sections, devices, tiles, source, frame),
        out_shape=(
            jax.ShapeDtypeStruct((bands, BAND, frame), BF16),
            jax.ShapeDtypeStruct((GRADS, 1, tiles), F32),
        ),
        in_specs=[any_space] * 6,
        out_specs=(any_space, pl.BlockSpec(memory_space=pltpu.VMEM)),
        scratch_shapes=[
            smem((2, all_tiles), F32),
            smem((2, all_tiles), F32),
            smem((2, all_tiles), jnp.int32),
            smem((devices, 128), jnp.int32),
            vmem((devices, 128), jnp.int32),
            vmem((devices, 128), jnp.int32),
            vmem((tiles, source, source), BF16),
            vmem((rows, BAND, frame), BF16),
            vmem((devices, 2, BAND, frame), BF16),
            vmem((devices, 2, BAND, frame), BF16),
            vmem((devices, 2, BAND, frame), F32),
            vmem((devices, 2, BAND, frame), BF16),
            vmem((devices, 2, BAND, frame), BF16),
            vmem((devices, 2, BAND, frame), F32),
            vmem((devices * 2 * BAND // 256, frame, 256), BF16),
            vmem((bands, BAND, frame), BF16),
            vmem((bands, BAND, frame), BF16),
            vmem((2, GRADS, devices, 8, 128), F32),
            vmem((devices, 128), F32),
            vmem((devices, 1, 128), F32),
            vmem((devices, 1, 128), F32),
            vmem((1, 128), F32),
            vmem((pairs, 1, 128), F32),
            vmem((pairs, 128), F32),
            vmem((chips, pairs, 128), F32),
            vmem((128, chips * pairs), F32),
            sem((3,)),
            sem,
            sem((tiles,)),
            sem,
            sem,
            sem,
            sem((devices,)),
            sem((devices,)),
            sem,
            sem,
            sem((devices,)),
            sem((devices,)),
            sem((pairs,)),
            sem((pairs,)),
            sem((chips,)),
            sem((chips,)),
        ],
        compiler_params=pltpu.CompilerParams(
            collective_id=0, has_side_effects=True, vmem_limit_bytes=48 << 20
        ),
    )(
        zoom[0],
        frac[0],
        offset[0],
        routes,
        patches[0],
        top_grid.reshape(bands, BAND, frame),
    )
    return (grid.reshape(1, 1, frame, frame), corrections)


def solution(mesh):
    placed = (
        P("sec", "tile", None, None),
        P("sec", None, None),
        P("sec", None, None),
        P("sec", None, None),
        P("sec", None, None, None),
        P("tile", None, None),
    )
    return jax.shard_map(
        shards,
        mesh=mesh,
        in_specs=placed,
        out_specs=(P("sec", "tile", None, None), P(None, "sec", "tile")),
        check_vma=False,
    )
```

```python
import functools

import jax
import jax.numpy as jnp
from jax import lax
from jax.experimental import pallas as pl
from jax.experimental.pallas import tpu as pltpu
from jax.sharding import PartitionSpec as P

BAND = 16
ITERS = 2
COUPLING = 0.25
MESH = pl.DeviceIdType.MESH
F32 = jnp.float32
BF16 = jnp.bfloat16

MONOMIALS = ((0, 0), (1, 0), (0, 1), (2, 0), (1, 1), (0, 2))
PAIR = ((0, 1, 2), (1, 3, 4), (2, 4, 5))
GRADS = 6


def moment_of(f, g):
    return (f // 3 + g // 3) * 6 + PAIR[f % 3][g % 3]


def iota(shape, dim):
    return lax.broadcasted_iota(jnp.int32, shape, dim)


def fiota(shape, dim):
    return iota(shape, dim).astype(F32)


def shifted(x, distance):
    width = x.shape[1]
    return pltpu.roll(x, (-distance) % width, 1)


def total(x):
    return jnp.sum(jnp.sum(x, axis=0, keepdims=True), axis=1, keepdims=True)


def kernel(
    sections, devices, tiles, source, frame,
    zoom_hbm, frac_hbm, offset_hbm, routes_hbm, patch_hbm, top_hbm,
    grid_hbm, corr_ref,
    zoom_s, frac_s, offset_s, tab_s, tab_v, routes_v,
    patch_v, rendered, outgoing, incoming, weights, weights_hi, weights_lo, lit,
    select, grid_v, above, partial, home, mine_sums, all_sums, pair_sums, all_pairs, right_v,
    mom_row, mom_rows, mom_turned, mom_mine, mom_all,
    param_sem, route_sem, patch_sem, tab_sem, top_sem, out_sem,
    send_a, recv_a, send_g, recv_g, send_m, recv_m, send_x, recv_x, send_p, recv_p, send_c, recv_c,
):
    bands = frame // BAND
    rows = tiles * bands
    me_sec = lax.axis_index("sec")
    me = lax.axis_index("tile")
    chip, core = me // 2, me % 2
    chips = devices // 2
    half = frame // 2
    middle = (frame - 1) / 2.0

    params = [
        pltpu.make_async_copy(a, b, param_sem.at[n])
        for n, (a, b) in enumerate(((zoom_hbm, zoom_s), (frac_hbm, frac_s), (offset_hbm, offset_s)))
    ]
    route_copy = pltpu.make_async_copy(routes_hbm, routes_v, route_sem)
    route_copy.start()
    for c in params:
        c.start()

    def patch_copy(t):
        return pltpu.make_async_copy(patch_hbm.at[t], patch_v.at[t], patch_sem.at[t])

    for t in range(tiles):
        patch_copy(t).start()
    top_copy = pltpu.make_async_copy(top_hbm, above, top_sem)

    @pl.when(me_sec == sections - 1)
    def _():
        top_copy.start()

    barrier = pltpu.get_barrier_semaphore()

    def greet(d, carry):
        pl.semaphore_signal(
            barrier, 1, device_id=(me_sec, lax.rem(me + d, devices)), device_id_type=MESH
        )
        return carry

    lax.fori_loop(1, devices, greet, 0)
    pair_peers = [
        (lax.rem(me_sec + ds, sections), chip * 2 + lax.rem(core + dc, 2))
        for ds in range(sections)
        for dc in range(2)
        if ds or dc
    ]
    for n, peer in enumerate(pair_peers):
        if n:
            pl.semaphore_signal(barrier, 1, device_id=peer, device_id_type=MESH)

    route_copy.wait()
    lane = iota((devices, 128), 1)
    mine = (routes_v[...] == me) & (lane < rows)
    take0 = jnp.min(jnp.where(mine, lane, rows - 1), axis=1, keepdims=True)
    take1 = jnp.max(jnp.where(mine, lane, 0), axis=1, keepdims=True)
    count = jnp.sum(jnp.where(mine, 1, 0), axis=1, keepdims=True)
    own_row = routes_v[pl.ds(me, 1), :]
    hit = (own_row == iota((devices, 128), 0)) & (lane < rows)
    out0 = jnp.min(jnp.where(hit, lane, rows - 1), axis=1, keepdims=True)
    out1 = jnp.max(jnp.where(hit, lane, 0), axis=1, keepdims=True)
    valid0 = count > 0
    valid1 = count > 1
    idx0, idx1 = take0, take1
    on0 = valid0.astype(jnp.int32)
    on1 = valid1.astype(jnp.int32)
    table = jnp.where(lane == 0, idx0, 0)
    table = jnp.where(lane == 1, idx1, table)
    table = jnp.where(lane == 2, out0, table)
    table = jnp.where(lane == 3, out1, table)
    table = jnp.where(lane == 4, on0, table)
    table = jnp.where(lane == 5, on1, table)
    tab_v[...] = table
    tab_copy = pltpu.make_async_copy(tab_v, tab_s, tab_sem)
    tab_copy.start()
    for c in params:
        c.wait()

    def scale_of(a, i):
        return zoom_s[a, i] * (frame / source)

    def points_of(spots, a, i):
        return (spots - offset_s[a, i].astype(F32) - frac_s[a, i]) / scale_of(a, i)

    def cover_of(points):
        return jnp.clip(jnp.minimum(points + 1.0, source - points), 0.0, 1.0)

    def hat(distance):
        return jnp.maximum(0.0, 1.0 - jnp.abs(distance)).astype(BF16)

    def render(t, carry):
        i = me * tiles + t
        down = points_of(fiota((frame, 128), 0), 0, i)
        down = jnp.concatenate([down] * (source // 128), axis=1)
        row_weights = hat(down - fiota((frame, source), 1))
        across = points_of(fiota((8, frame), 1), 1, i)
        across = jnp.broadcast_to(across[0:1], (source, frame))
        col_weights = hat(across - fiota((source, frame), 0))
        patch_copy(t).wait()
        halfway = jnp.dot(row_weights, patch_v[t], preferred_element_type=F32).astype(BF16)
        image = jnp.dot(halfway, col_weights, preferred_element_type=F32).astype(BF16)
        rendered[pl.ds(pl.multiple_of(t * bands, bands), bands)] = image.reshape(bands, BAND, frame)
        return carry

    lax.fori_loop(0, tiles, render, 0)

    tab_copy.wait()

    def pack(g, carry):
        outgoing[g, 0] = rendered[tab_s[g, 2] & (rows - 1)]
        outgoing[g, 1] = rendered[tab_s[g, 3] & (rows - 1)]
        return carry

    lax.fori_loop(0, devices, pack, 0)
    incoming[me] = outgoing[me]
    greeted = devices - 1 + len(pair_peers) - 1
    pl.semaphore_wait(barrier, greeted)

    def band_copy(peer, from_):
        return pltpu.make_async_remote_copy(
            src_ref=outgoing.at[peer],
            dst_ref=incoming.at[from_],
            send_sem=send_a.at[peer],
            recv_sem=recv_a.at[from_],
            device_id=(me_sec, peer),
            device_id_type=MESH,
        )

    def send_bands(d, carry):
        band_copy(lax.rem(me + d, devices), me).start()
        return carry

    lax.fori_loop(1, devices, send_bands, 0)

    def cover_slot(j, carry):
        for c in range(2):
            idx = tab_s[j, c] & (rows - 1)
            i = j * tiles + (idx >> 4)
            k = idx & (bands - 1)
            start = (k * BAND).astype(F32)
            down = cover_of(points_of(fiota((BAND, 128), 0) + start, 0, i))
            down = down * (tab_s[j, 4 + c].astype(F32) / (frame * frame))
            across = cover_of(points_of(fiota((8, frame), 1), 1, i))
            weight = jnp.concatenate([down, down], axis=1) * jnp.broadcast_to(
                across[0:1], (BAND, frame)
            )
            weights[j, c] = weight
            hi = weight.astype(BF16)
            weights_hi[j, c] = hi
            weights_lo[j, c] = (weight - hi.astype(F32)).astype(BF16)
        return carry

    lax.fori_loop(0, devices, cover_slot, 0)

    sub = iota((devices, 128), 0)
    band0 = jnp.where(valid0, (idx0 & (bands - 1)).astype(F32), -float(bands))
    band1 = jnp.where(valid1, (idx1 & (bands - 1)).astype(F32), -float(bands))
    along = jnp.where(lane == sub, band0, 0.0) + jnp.where(lane == sub + devices, band1, 0.0)
    along = jnp.broadcast_to(jnp.sum(along, axis=0, keepdims=True), (8, 128)).astype(BF16)
    chunk = 256 // (2 * BAND)
    chunks = devices // chunk
    wide = iota((128, 256), 1)

    def choose(h, cover):
        spread = (iota((128, 256), 0) == h * chunk + wide // (2 * BAND) + devices * ((wide // BAND) % 2))
        spread = jnp.where(spread, 1.0, 0.0).astype(BF16)
        target = jnp.dot(along, spread, preferred_element_type=F32)[0:1]
        target = target * BAND + (iota((1, 256), 1) % BAND).astype(F32)
        onehot = jnp.where(fiota((frame, 256), 0) == target, 1.0, 0.0).astype(BF16)
        select[h] = onehot
        at = pl.ds(pl.multiple_of(h * chunk, chunk), chunk)
        cover += jnp.dot(onehot, weights_hi[at].reshape(256, frame), preferred_element_type=F32)
        cover += jnp.dot(onehot, weights_lo[at].reshape(256, frame), preferred_element_type=F32)
        return cover

    cover = lax.fori_loop(0, chunks, choose, jnp.zeros((frame, frame), F32))
    cover = 1.0 + cover * float(frame * frame)

    def locate(n, carry):
        first, second = carry
        theirs = (routes_v[...] == 2 * n + core) & (lane < rows)
        low = jnp.min(jnp.where(theirs, lane, rows - 1), axis=1, keepdims=True)
        high = jnp.max(jnp.where(theirs, lane, 0), axis=1, keepdims=True)
        named = jnp.sum(jnp.where(theirs, 1, 0), axis=1, keepdims=True)
        low = jnp.where(named > 0, low >> 4, -1)
        high = jnp.where(named > 1, high >> 4, -1)
        return jnp.where(lane == n, low, first), jnp.where(lane == n, high, second)

    nowhere = jnp.zeros((devices, 128), jnp.int32)
    first, second = lax.fori_loop(0, chips, locate, (nowhere, nowhere))
    where = jnp.transpose(jnp.concatenate([first, second], axis=0).astype(F32))
    for n in range(chips):
        home[n] = jnp.broadcast_to(where[n : n + 1], (8, 128))

    row_lane = iota((1, 128), 1)

    def moments(t, payload):
        i = me * tiles + t
        down = cover_of(points_of(fiota((frame, 128), 0), 0, i)) / (frame * frame)
        y = (fiota((frame, 128), 0) - middle) / (frame / 2.0)
        down = [jnp.concatenate([v, v], axis=1) for v in (down, down * y, down * y * y)]
        across = cover_of(points_of(fiota((8, frame), 1), 1, i))[0:1]
        x = (fiota((1, frame), 1) - middle) / (frame / 2.0)
        across = (across, across * x, across * x * x)
        at = pl.ds(pl.multiple_of(t * bands, bands), bands)
        level = rendered[at].reshape(frame, frame).astype(F32)
        for p, image in enumerate((None, level, level * level)):
            for b in range(3):
                column = down[b] if image is None else down[b] * image
                column = jnp.sum(column, axis=0, keepdims=True)
                for m, (a, b2) in enumerate(MONOMIALS):
                    if b2 == b:
                        value = jnp.sum(column * across[a], axis=1, keepdims=True)
                        payload = jnp.where(
                            row_lane == (p * 6 + m) * tiles + t, value, payload
                        )
        return payload

    own = lax.fori_loop(0, tiles, moments, jnp.zeros((1, 128), F32))
    mom_row[...] = own
    mom_rows[me] = own

    def moment_copy(peer, from_):
        return pltpu.make_async_remote_copy(
            src_ref=mom_row,
            dst_ref=mom_rows.at[from_],
            send_sem=send_m.at[peer],
            recv_sem=recv_m.at[from_],
            device_id=(me_sec, peer),
            device_id_type=MESH,
        )

    def send_moments(d, carry):
        moment_copy(lax.rem(me + d, devices), me).start()
        return carry

    lax.fori_loop(1, devices, send_moments, 0)

    grid = jnp.zeros((frame, frame), F32)

    def arrive(h, grid):
        def one(n, carry):
            j = h * chunk + n

            @pl.when(j != me)
            def _():
                band_copy(j, j).wait_recv()

            return carry

        lax.fori_loop(0, chunk, one, 0)
        at = pl.ds(pl.multiple_of(h * chunk, chunk), chunk)
        return grid + jnp.dot(
            select[h], incoming[at].reshape(256, frame), preferred_element_type=F32
        )

    grid = lax.fori_loop(0, chunks, arrive, grid)
    grid_v[...] = (grid / cover).astype(BF16).reshape(bands, BAND, frame)
    write_grid = pltpu.make_async_copy(grid_v, grid_hbm, out_sem)
    write_grid.start()
    to_below = pltpu.make_async_remote_copy(
        src_ref=grid_v,
        dst_ref=above,
        send_sem=send_g,
        recv_sem=recv_g,
        device_id=(lax.rem(me_sec + sections - 1, sections), me),
        device_id_type=MESH,
    )

    @pl.when(me_sec > 0)
    def _():
        to_below.start()

    def weigh(j, carry):
        for c in range(2):
            lit[j, c] = weights[j, c] * incoming[j, c].astype(F32)
        return carry

    lax.fori_loop(0, devices, weigh, 0)

    def await_moments(d, carry):
        j = lax.rem(me + d, devices)
        moment_copy(j, j).wait_recv()
        return carry

    lax.fori_loop(1, devices, await_moments, 0)
    turned = jnp.concatenate([mom_rows[:, 0, :], jnp.zeros((devices, 128), F32)], axis=0)
    mom_turned[...] = jnp.transpose(turned)
    for h in range(2):
        even, odd = (mom_turned[pl.ds(2 * h + n, 24, stride=tiles), :] for n in range(2))
        mom_mine[h] = even + pltpu.roll(odd, devices, 1)
    mom_all[me_sec] = mom_mine[...]

    def section_copy(ds, from_):
        return pltpu.make_async_remote_copy(
            src_ref=mom_mine,
            dst_ref=mom_all.at[from_],
            send_sem=send_x.at[ds],
            recv_sem=recv_x.at[from_],
            device_id=(lax.rem(me_sec + ds, sections), me),
            device_id_type=MESH,
        )

    for ds in range(1, sections):
        section_copy(ds, me_sec).start()

    @pl.when(me_sec < sections - 1)
    def _():
        to_below.wait_recv()

    @pl.when(me_sec == sections - 1)
    def _():
        top_copy.wait()

    x = (fiota((8, frame), 1) - middle) / (frame / 2.0)
    x0, x1 = x[:, :half], x[:, half:]
    y_base = (fiota((BAND, half), 0) - middle) / (frame / 2.0)

    def contract(j, carry):
        for c in range(2):
            k = tab_s[j, c] & (bands - 1)
            target = above[k].astype(F32)
            y = y_base + (k * BAND).astype(F32) / (frame / 2.0)
            for n, factor in enumerate((weights, lit)):
                product = target * factor[j, c]
                left, right = product[:, :half], product[:, half:]
                both = left + right
                left, right = left[:8] + left[8:], right[:8] + right[8:]
                y_part = both * y
                partial[c, n * 3, j] = left + right
                partial[c, n * 3 + 1, j] = left * x0 + right * x1
                partial[c, n * 3 + 2, j] = y_part[:8] + y_part[8:]
        return carry

    lax.fori_loop(0, devices, contract, 0)
    answers = []
    for c in range(2):
        answer = jnp.zeros((devices, 128), F32)
        for f in range(GRADS):
            value = jnp.sum(jnp.sum(partial[c, f], axis=1), axis=1, keepdims=True)
            answer = jnp.where(lane == f, value, answer)
        answers.append(answer)
    mine_sums[...] = jnp.transpose(jnp.concatenate(answers, axis=0))[:8]
    all_sums[chip] = mine_sums[...]

    def chip_copy(other, from_):
        return pltpu.make_async_remote_copy(
            src_ref=mine_sums,
            dst_ref=all_sums.at[from_],
            send_sem=send_c.at[other],
            recv_sem=recv_c.at[from_],
            device_id=(me_sec, other * 2 + core),
            device_id_type=MESH,
        )

    def send_rows(d, carry):
        chip_copy(lax.rem(chip + d, chips), chip).start()
        return carry

    lax.fori_loop(1, chips, send_rows, 0)

    def await_rows(d, carry):
        j = lax.rem(chip + d, chips)
        chip_copy(j, j).wait_recv()
        return carry

    lax.fori_loop(1, chips, await_rows, 0)

    row_id, lane_id = iota((8, 128), 0), iota((8, 128), 1)
    left_side = lane_id < devices
    by_tile = []
    for t in range(tiles):
        added = jnp.sum(jnp.where(home[...] == float(t), all_sums[...], 0.0), axis=0)
        by_tile.append(added + pltpu.roll(added, devices, 1))
    place = me_sec * 2 + core
    for h in range(2):
        pair_sums[h] = jnp.where(left_side, by_tile[2 * h], by_tile[2 * h + 1])
    all_pairs[place] = pair_sums[...]

    def pair_copy(n, peer, from_):
        return pltpu.make_async_remote_copy(
            src_ref=pair_sums,
            dst_ref=all_pairs.at[from_],
            send_sem=send_p.at[n],
            recv_sem=recv_p.at[from_],
            device_id=peer,
            device_id_type=MESH,
        )

    for n, peer in enumerate(pair_peers):
        pair_copy(n, peer, place).start()
    for ds in range(1, sections):
        s = lax.rem(me_sec + ds, sections)
        section_copy(ds, s).wait_recv()
    for n, peer in enumerate(pair_peers):
        pair_copy(n, peer, peer[0] * 2 + lax.rem(peer[1], 2)).wait_recv()
    for s in range(sections):
        for h in range(2):
            right_v[2 * s + h] = all_pairs[2 * s, h] + all_pairs[2 * s + 1, h]

    shape = (8, 128)
    moment = [mom_all[:, :, m, :].reshape(shape) for m in range(18)]
    right_side = [right_v[:, f, :] - moment[moment_of(f, 3)] for f in range(GRADS)]
    precond = [1.0 / (moment[moment_of(f, f)] + 4.0 * COUPLING) for f in range(GRADS)]
    upper_pair = (row_id & 1) == 1
    device_id = lane_id & (devices - 1)

    def beside_of(d):
        across = pltpu.roll(d, devices, 1)
        after = jnp.where(
            upper_pair,
            jnp.where(device_id < devices - 1, pltpu.roll(shifted(across, 1), 1, 0), 0.0),
            pltpu.roll(across, 7, 0),
        )
        after = jnp.where(left_side, across, after)
        before = jnp.where(
            upper_pair,
            pltpu.roll(across, 1, 0),
            jnp.where(device_id > 0, pltpu.roll(shifted(across, -1), 7, 0), 0.0),
        )
        before = jnp.where(left_side, before, across)
        upper = jnp.where(row_id < 6, pltpu.roll(d, 6, 0), 0.0)
        lower = jnp.where(row_id >= 2, pltpu.roll(d, 2, 0), 0.0)
        return upper + lower + after + before

    def inner(left, right):
        return total(sum(a * b for a, b in zip(left, right)))

    residual = right_side
    scaled = [p * r for p, r in zip(precond, residual)]
    direction = scaled
    current = inner(residual, scaled)
    result = [jnp.zeros(shape, F32)] * GRADS
    for step in range(ITERS):
        image = [
            sum(moment[moment_of(f, g)] * direction[g] for g in range(GRADS))
            + COUPLING * (4.0 * direction[f] - beside_of(direction[f]))
            for f in range(GRADS)
        ]
        alpha = current / inner(direction, image)
        result = [c + alpha * d for c, d in zip(result, direction)]
        if step + 1 < ITERS:
            residual = [r - alpha * h for r, h in zip(residual, image)]
            scaled = [p * r for p, r in zip(precond, residual)]
            following = inner(residual, scaled)
            ratio = following / current
            direction = [z + ratio * d for z, d in zip(scaled, direction)]
            current = following
    own_device = device_id == me
    first_lanes = iota((1, 128), 1)
    for f in range(GRADS):
        line = jnp.zeros((1, 128), F32)
        for t in range(tiles):
            spot = own_device & (row_id == me_sec * 2 + t // 2) & (left_side == (t % 2 == 0))
            line = jnp.where(first_lanes == t, total(jnp.where(spot, result[f], 0.0)), line)
        corr_ref[f] = line[:, :tiles]

    def sent(d, carry):
        peer = lax.rem(me + d, devices)
        band_copy(peer, me).wait_send()
        moment_copy(peer, me).wait_send()
        return carry

    lax.fori_loop(1, devices, sent, 0)

    def sent_rows(d, carry):
        chip_copy(lax.rem(chip + d, chips), chip).wait_send()
        return carry

    lax.fori_loop(1, chips, sent_rows, 0)
    for ds in range(1, sections):
        section_copy(ds, me_sec).wait_send()
    for n, peer in enumerate(pair_peers):
        pair_copy(n, peer, place).wait_send()

    @pl.when(me_sec > 0)
    def _():
        to_below.wait_send()

    write_grid.wait()


def shards(patches, zoom, frac, offset, owner, top_grid):
    _, tiles, source, _ = patches.shape
    frame = top_grid.shape[1]
    sections, devices = lax.axis_size("sec"), lax.axis_size("tile")
    bands = frame // BAND
    rows = tiles * bands
    chips = devices // 2
    pairs = 2 * sections
    routes = jnp.pad(owner.reshape(devices, rows), ((0, 0), (0, 128 - rows)))
    any_space = pl.BlockSpec(memory_space=pl.ANY)
    vmem, smem, sem = pltpu.VMEM, pltpu.SMEM, pltpu.SemaphoreType.DMA
    all_tiles = tiles * devices
    grid, corrections = pl.pallas_call(
        functools.partial(kernel, sections, devices, tiles, source, frame),
        out_shape=(
            jax.ShapeDtypeStruct((bands, BAND, frame), BF16),
            jax.ShapeDtypeStruct((GRADS, 1, tiles), F32),
        ),
        in_specs=[any_space] * 6,
        out_specs=(any_space, pl.BlockSpec(memory_space=pltpu.VMEM)),
        scratch_shapes=[
            smem((2, all_tiles), F32),
            smem((2, all_tiles), F32),
            smem((2, all_tiles), jnp.int32),
            smem((devices, 128), jnp.int32),
            vmem((devices, 128), jnp.int32),
            vmem((devices, 128), jnp.int32),
            vmem((tiles, source, source), BF16),
            vmem((rows, BAND, frame), BF16),
            vmem((devices, 2, BAND, frame), BF16),
            vmem((devices, 2, BAND, frame), BF16),
            vmem((devices, 2, BAND, frame), F32),
            vmem((devices, 2, BAND, frame), BF16),
            vmem((devices, 2, BAND, frame), BF16),
            vmem((devices, 2, BAND, frame), F32),
            vmem((devices * 2 * BAND // 256, frame, 256), BF16),
            vmem((bands, BAND, frame), BF16),
            vmem((bands, BAND, frame), BF16),
            vmem((2, GRADS, devices, 8, 128), F32),
            vmem((chips, 8, 128), F32),
            vmem((8, 128), F32),
            vmem((chips, 8, 128), F32),
            vmem((2, 8, 128), F32),
            vmem((pairs, 2, 8, 128), F32),
            vmem((2 * sections, 8, 128), F32),
            vmem((1, 128), F32),
            vmem((devices, 1, 128), F32),
            vmem((128, 128), F32),
            vmem((2, 24, 128), F32),
            vmem((sections, 2, 24, 128), F32),
            sem((3,)),
            sem,
            sem((tiles,)),
            sem,
            sem,
            sem,
            sem((devices,)),
            sem((devices,)),
            sem,
            sem,
            sem((devices,)),
            sem((devices,)),
            sem((sections,)),
            sem((sections,)),
            sem((pairs,)),
            sem((pairs,)),
            sem((chips,)),
            sem((chips,)),
        ],
        compiler_params=pltpu.CompilerParams(
            collective_id=0, has_side_effects=True, vmem_limit_bytes=63 << 20
        ),
    )(
        zoom[0],
        frac[0],
        offset[0],
        routes,
        patches[0],
        top_grid.reshape(bands, BAND, frame),
    )
    return (grid.reshape(1, 1, frame, frame), corrections)


def solution(mesh):
    placed = (
        P("sec", "tile", None, None),
        P("sec", None, None),
        P("sec", None, None),
        P("sec", None, None),
        P("sec", None, None, None),
        P("tile", None, None),
    )
    return jax.shard_map(
        shards,
        mesh=mesh,
        in_specs=placed,
        out_specs=(P("sec", "tile", None, None), P(None, "sec", "tile")),
        check_vma=False,
    )
```
